32 devices in a mesh: grp: 8 (over z, x), ulys: 4 (over y, core).
Axes of the slice: x: 2, y: 2, z: 4, core: 2. Of those that a mesh axis runs over, the one named last changes fastest.
Arguments:
- query_in: bfloat16 [4096, 2048], P(('grp', 'ulys')), may hold values from -3 to 3
- key_in: bfloat16 [4096, 2048], P(('grp', 'ulys')), may hold values from -3 to 3
- value_in: bfloat16 [4096, 2048], P(('grp', 'ulys')), may hold values from -6 to 6
- grad_out: bfloat16 [4096, 2048], P(('grp', 'ulys')), may hold values from -6 to 6
- fwd_out: bfloat16 [4096, 2048], P(('grp', 'ulys')), may hold values from -6 to 6
- log_norm: float32 [4096, 32], P(('grp', 'ulys')), may hold values from 3 to 5
- sample_len: int32 [8, 4], P('grp'), may hold values from 1 to 256, 512 in all within a row
- plan_offset: int32 [8, 4], P('grp'), may hold values from -1 to 1, as said below
Outputs:
- grad_query: bfloat16 [4096, 2048], P(('grp', 'ulys'))
- grad_key: bfloat16 [4096, 2048], P(('grp', 'ulys'))
- grad_value: bfloat16 [4096, 2048], P(('grp', 'ulys'))
The draws below stay inside these ranges and needn't reach their ends.
Inputs may be any that keep to these rules, and one draw needn't show every extreme that they name: `sample_len`: row g lists the sample lengths of pack g; it sums to 512 and its largest entry is 256. `plan_offset`: entry [g, u] = d names block (g + d, u) of an existing group, and entry [g + d, u] is -d, so each column is a permutation of the groups made of swaps of neighbours.
All inputs are finite; a program needn't handle non-finite values.
Results may differ from the reference program's by a relative error of at most 0.012.
Values may be sent and summed in bfloat16 or wider, within the bound.
A program may use at most 128 MiB of HBM per device.

```python
import math
import jax
import jax.numpy as jnp
import numpy as np
from jax import lax

HEADS = 32
HEAD_DIM = 64
TOK_DEV = 128
NSAMP = 4
GROUP_TOK = 512
MOST_LEN = 256
TOKENS = 4096
N_GRP = 8
N_ULYS = 4


def draw_plan_offset(key, part):
    key_parity, key_gate = jax.random.split(key)
    parity = jax.random.randint(key_parity, (N_ULYS,), 0, 2).astype(jnp.int32)
    parity = parity.at[0].set(0).at[1].set(1)
    gate = jax.random.randint(key_gate, (N_ULYS, N_GRP), 0, 2).astype(jnp.int32)
    gate = gate.at[0].set(1).at[1].set(1)
    groups = lax.iota(jnp.int32, N_GRP)[None, :]
    phase = (groups - parity[:, None]) % 2
    left_side = (phase == 0) & (groups + 1 < N_GRP)
    right_side = (phase == 1) & (groups - 1 >= 0)
    gate_right = jnp.roll(gate, 1, axis=1)
    offsets = jnp.where(left_side & (gate == 1), 1, jnp.where(right_side & (gate_right == 1), -1, 0))
    return jnp.transpose(offsets).astype(jnp.int32)


def level_of(stream_key, shape, pieces, smallest, largest):
    def one(dim, blocks):
        steps = jax.random.uniform(jax.random.fold_in(jax.random.fold_in(stream_key, 6), dim), (blocks,), jnp.float32, smallest / len(pieces), largest / len(pieces))
        return jnp.repeat(jnp.exp(steps), shape[dim] // blocks).reshape((-1,) + (1,) * (len(shape) - dim - 1))

    gain = one(*pieces[0])
    for cut in pieces[1:]:
        gain = gain * one(*cut)
    return gain


def profile(count, total, reach, slope):
    weights = [(1 << 20) // math.isqrt(standing ** slope) + 1 for standing in range(2, count + 1)]
    spare, holding = total - reach - (count - 1), [1] * (count - 1)
    while spare > 0:
        movable = [i for i in range(count - 1) if holding[i] < reach]
        whole, budget = sum([weights[i] for i in movable]), spare
        for i in movable:
            addition = min(reach - holding[i], max(1, budget * weights[i] // whole), spare)
            holding[i] = holding[i] + addition
            spare = spare - addition
    return np.array([reach] + holding)


def uneven_parts(rng, number_of, total, limit, slope):
    if number_of == 2:
        one = jax.random.randint(rng, (), max(1, total - limit), min(limit, total - 1) + 1)
        return jnp.stack([one, total - one])
    sizes = jnp.asarray(profile(number_of, total, limit, slope), jnp.int32)
    pairs = (number_of - 1) // 2
    source_of, sink = sizes[1:1 + 2 * pairs:2], sizes[2:2 + 2 * pairs:2]
    margin = jnp.minimum(source_of - 1, limit - sink)
    shifted = jax.random.randint(jax.random.fold_in(rng, 1), (pairs,), 0, 1 << 20) % (margin + 1)
    sizes = sizes.at[1:1 + 2 * pairs:2].set(source_of - shifted).at[2:2 + 2 * pairs:2].set(sink + shifted)
    return sizes[jax.random.permutation(jax.random.fold_in(rng, 2), number_of)]


def normal_values(own_key, dims, scale, most, cuts=(), held_as=jnp.bfloat16):
    array = jax.random.normal(own_key, dims, jnp.float32) * scale
    if len(cuts) > 0:
        array = level_of(own_key, dims, cuts, -0.22, 0.18) * array
    return jnp.clip(array, min=-most, max=most).astype(held_as)


def setup_inputs(seed: int = 0) -> dict:
    seeds = jax.random.split(jax.random.key(seed), 9)
    return {
        "query_in": normal_values(seeds[0], (TOKENS, HEADS * HEAD_DIM), 0.7, 3.0, ((0, 32),)),
        "key_in": normal_values(seeds[1], (TOKENS, HEADS * HEAD_DIM), 0.7, 3.0, ((0, 32),)),
        "value_in": normal_values(seeds[2], (TOKENS, HEADS * HEAD_DIM), 1.0, 6.0, ((0, 32),)),
        "grad_out": normal_values(seeds[3], (TOKENS, HEADS * HEAD_DIM), 1.0, 6.0, ((0, 32),)),
        "fwd_out": normal_values(seeds[4], (TOKENS, HEADS * HEAD_DIM), 1.0, 6.0, ((0, 32),)),
        "log_norm": jnp.clip(3.0 + 2.0 * jax.random.uniform(seeds[5], (TOKENS, HEADS), jnp.float32) ** level_of(seeds[5], (TOKENS, HEADS), ((0, 32),), -0.2, 0.2), 3.0, 5.0),
        "sample_len": jax.vmap(lambda own: uneven_parts(own, NSAMP, GROUP_TOK, MOST_LEN, 2))(jax.random.split(seeds[6], N_GRP)).reshape((N_GRP, NSAMP)).astype(jnp.int32),
        "plan_offset": draw_plan_offset(jax.random.fold_in(seeds[8], 71), 0),
    }


def rotate_half(values):
    half_dim = values.shape[1] // 2
    return jnp.concatenate([-values[:, half_dim:], values[:, :half_dim]], axis=1)


def rotate_back(values):
    half_dim = values.shape[1] // 2
    return jnp.concatenate([values[:, half_dim:], -values[:, :half_dim]], axis=1)


def rope_tables(lengths_row, total_rows, head_dim):
    ends = jnp.cumsum(lengths_row)
    row_index = lax.broadcasted_iota(jnp.int32, (total_rows, 1), 0)
    passed = (row_index >= ends[None, :]).astype(jnp.int32)
    segment = jnp.sum(passed, axis=1)
    position = row_index[:, 0] - jnp.sum(passed * lengths_row[None, :], axis=1)
    half_dim = head_dim // 2
    freq = jnp.power(10000.0, -lax.iota(jnp.float32, half_dim) / half_dim)
    angle = position.astype(jnp.float32)[:, None] * freq[None, :]
    cosine = jnp.concatenate([jnp.cos(angle), jnp.cos(angle)], axis=1)
    sine = jnp.concatenate([jnp.sin(angle), jnp.sin(angle)], axis=1)
    return segment, cosine, sine


def head_grads(q_head, k_head, v_head, d_head, lse_head, delta_head, segment, cosine, sine):
    q_float = q_head.astype(jnp.float32)
    k_float = k_head.astype(jnp.float32)
    q_rot = (q_float * cosine + rotate_half(q_float) * sine).astype(jnp.bfloat16)
    k_rot = (k_float * cosine + rotate_half(k_float) * sine).astype(jnp.bfloat16)
    scores = jnp.dot(q_rot, k_rot.T, preferred_element_type=jnp.float32) * 0.125
    same_sample = segment[:, None] == segment[None, :]
    prob = jnp.where(same_sample, jnp.exp(scores - lse_head[:, None]), 0.0)
    prob_low = prob.astype(jnp.bfloat16)
    dprob = jnp.dot(d_head, v_head.T, preferred_element_type=jnp.float32)
    dscore = (prob * (dprob - delta_head[:, None])).astype(jnp.bfloat16)
    grad_v = jnp.dot(prob_low.T, d_head, preferred_element_type=jnp.float32)
    grad_qr = jnp.dot(dscore, k_rot, preferred_element_type=jnp.float32) * 0.125
    grad_kr = jnp.dot(dscore.T, q_rot, preferred_element_type=jnp.float32) * 0.125
    grad_q = grad_qr * cosine + rotate_back(grad_qr * sine)
    grad_k = grad_kr * cosine + rotate_back(grad_kr * sine)
    return grad_q.astype(jnp.bfloat16), grad_k.astype(jnp.bfloat16), grad_v.astype(jnp.bfloat16)


def reference(query_in, key_in, value_in, grad_out, fwd_out, log_norm, sample_len, plan_offset):
    width = HEADS * HEAD_DIM
    group_rows = TOK_DEV * N_ULYS
    products = grad_out.astype(jnp.float32) * fwd_out.astype(jnp.float32)
    delta = jnp.sum(products.reshape(TOKENS, HEADS, HEAD_DIM), axis=2)

    def one_group(packed):
        q_group, k_group, v_group, d_group, lse_group, delta_group, lengths_row = packed
        segment, cosine, sine = rope_tables(lengths_row, group_rows, HEAD_DIM)
        q_list, k_list, v_list = [], [], []
        for head_idx in range(HEADS):
            lo_col = head_idx * HEAD_DIM
            hi_col = lo_col + HEAD_DIM
            grad_q, grad_k, grad_v = head_grads(q_group[:, lo_col:hi_col], k_group[:, lo_col:hi_col],
                                                v_group[:, lo_col:hi_col], d_group[:, lo_col:hi_col],
                                                lse_group[:, head_idx], delta_group[:, head_idx],
                                                segment, cosine, sine)
            q_list.append(grad_q)
            k_list.append(grad_k)
            v_list.append(grad_v)
        return (jnp.concatenate(q_list, axis=1), jnp.concatenate(k_list, axis=1), jnp.concatenate(v_list, axis=1))

    packed = (query_in.reshape(N_GRP, group_rows, width), key_in.reshape(N_GRP, group_rows, width),
              value_in.reshape(N_GRP, group_rows, width), grad_out.reshape(N_GRP, group_rows, width),
              log_norm.reshape(N_GRP, group_rows, HEADS), delta.reshape(N_GRP, group_rows, HEADS), sample_len)
    grads = lax.map(one_group, packed)
    source = (lax.iota(jnp.int32, N_GRP)[:, None] + plan_offset).astype(jnp.int32)
    ulys_ids = lax.iota(jnp.int32, N_ULYS)[None, :]
    routed = []
    for grad_all in grads:
        blocks = grad_all.reshape(N_GRP, N_ULYS, TOK_DEV, width)
        routed.append(blocks[source, ulys_ids].reshape(TOKENS, width))
    return (routed[0], routed[1], routed[2])
```

```python
import functools

import jax
import jax.numpy as jnp
import numpy as np
from jax import lax
from jax.experimental import pallas as pl
from jax.experimental.pallas import tpu as pltpu
from jax.sharding import PartitionSpec as P

MESH = pl.DeviceIdType.MESH
LANES = 128
NT = (((1,), (1,)), ((), ()))
TN = (((0,), (0,)), ((), ()))


def swap_halves(x, low, half):
    return jnp.where(low, pltpu.roll(x, LANES - half, 1), pltpu.roll(x, half, 1))


def kernel(
    n, groups, head_dim,
    freq_ref, len_ref, plan_ref, lse_ref, q_ref, k_ref, v_ref, d_ref, f_ref,
    oq_ref, ok_ref, ov_ref,
    stage, in_buf, f_vm, stat_out, stat_in, stat, cos_t, sin_t, bias,
    qs, kr, dq, grads, home, pair, relay,
    in_send, in_recv, st_send, st_recv, y_send, y_recv, x_send, x_recv, z_send, z_recv,
    loc_sem, df_sem,
):
    g = lax.axis_index("grp")
    me = lax.axis_index("ulys")
    heads_all, rows = lse_ref.shape
    heads = heads_all // n
    chunks = in_buf.shape[0]
    width = chunks * LANES
    per_chunk = LANES // head_dim
    half = head_dim // 2
    group_rows = n * rows
    blocks = n * chunks
    inputs = (q_ref, k_ref, v_ref, d_ref)

    even = lax.rem(g, 2) == 0
    partner = jnp.where(even, g + 1, g - 1)
    up, down = g + 2, g - 2
    has_up, has_down = up < groups, down >= 0
    z_to = jnp.where(even, up, down)
    has_to = jnp.where(even, up < groups, down >= 0)
    has_from = jnp.where(even, down >= 0, up < groups)

    barrier = pltpu.get_barrier_semaphore()
    near_w = jnp.where(lax.rem(me, 2) == 0, me + 1, me - 1)
    far = [lax.rem(near_w - lax.rem(near_w, 2) + o, n) for o in range(2, n)]
    others = far + [near_w]
    for w in others:
        pl.semaphore_signal(barrier, inc=1, device_id=(g, w), device_id_type=MESH)
    pl.semaphore_signal(barrier, inc=1, device_id=(partner, me), device_id_type=MESH)

    @pl.when(has_up)
    def _():
        pl.semaphore_signal(barrier, inc=1, device_id=(up, me), device_id_type=MESH)

    @pl.when(has_down)
    def _():
        pl.semaphore_signal(barrier, inc=1, device_id=(down, me), device_id_type=MESH)

    def load(p, t, w):
        return pltpu.make_async_copy(
            inputs[t].at[:, pl.ds(pl.multiple_of(w * width + p * LANES, LANES), LANES)],
            stage.at[p, w, t],
            loc_sem.at[p, t, w],
        )

    for p in range(chunks):
        for w in far + [near_w, me]:
            for t in range(4):
                load(p, t, w).start()
    copy_f = pltpu.make_async_copy(f_ref, f_vm, df_sem)
    copy_f.start()

    pl.semaphore_wait(barrier, n + has_up.astype(jnp.int32) + has_down.astype(jnp.int32))

    def in_copy(p, w, src):
        return pltpu.make_async_remote_copy(
            src_ref=stage.at[p, w],
            dst_ref=in_buf.at[p, src],
            send_sem=in_send.at[p, w],
            recv_sem=in_recv.at[p, src],
            device_id=(g, w),
            device_id_type=MESH,
        )

    def stat_copy(w, src):
        return pltpu.make_async_remote_copy(
            src_ref=stat_out.at[w], dst_ref=stat_in.at[src],
            send_sem=st_send.at[w], recv_sem=st_recv.at[src],
            device_id=(g, w), device_id_type=MESH,
        )

    def y_copy(p, w, src):
        return pltpu.make_async_remote_copy(
            src_ref=grads.at[p, w], dst_ref=home.at[src * chunks + p],
            send_sem=y_send.at[p, w], recv_sem=y_recv.at[p, src],
            device_id=(g, w), device_id_type=MESH,
        )

    def x_copy(b):
        return pltpu.make_async_remote_copy(
            src_ref=home.at[b], dst_ref=pair.at[b],
            send_sem=x_send.at[b], recv_sem=x_recv.at[b],
            device_id=(partner, me), device_id_type=MESH,
        )

    def z_copy(b):
        return pltpu.make_async_remote_copy(
            src_ref=pair.at[b], dst_ref=relay.at[b],
            send_sem=z_send.at[b], recv_sem=z_recv.at[b],
            device_id=(z_to, me), device_id_type=MESH,
        )

    for p in range(chunks):
        for w in others:
            for t in range(4):
                load(p, t, w).wait()
            if p == 0:
                in_copy(p, w, me).start()
        for t in range(4):
            load(p, t, me).wait()

    copy_f.wait()
    cols = f_vm.shape[1]
    d_full = jnp.concatenate([stage[p, w, 3] for w in range(n) for p in range(chunks)], axis=1)
    prod = d_full.astype(jnp.float32) * f_vm[...].astype(jnp.float32)
    high = prod.astype(jnp.bfloat16)
    rest = (prod - high.astype(jnp.float32)).astype(jnp.bfloat16)
    owner = lax.broadcasted_iota(jnp.int32, (heads_all, cols), 1) - head_dim * lax.broadcasted_iota(
        jnp.int32, (heads_all, cols), 0
    )
    pick = jnp.where((owner >= 0) & (owner < head_dim), 1.0, 0.0).astype(jnp.bfloat16)
    delta = lax.dot_general(pick, high, NT, preferred_element_type=jnp.float32)
    delta += lax.dot_general(pick, rest, NT, preferred_element_type=jnp.float32)
    lse = lse_ref[...]
    for w in range(n):
        stat_out[w, 0] = lse[w * heads:(w + 1) * heads]
        stat_out[w, 1] = delta[w * heads:(w + 1) * heads]
    for w in others:
        stat_copy(w, me).start()
    stat_in[me] = stat_out[me]

    lengths = [len_ref[0, s] for s in range(len_ref.shape[1])]
    ends = []
    for s, length in enumerate(lengths):
        ends.append(length if s == 0 else ends[-1] + length)
    lane = lax.broadcasted_iota(jnp.int32, (rows, LANES), 1)
    low = lax.rem(lane, head_dim) < half

    def segments(index):
        return sum((index >= e).astype(jnp.int32) for e in ends)

    seg_i = segments(lax.broadcasted_iota(jnp.int32, (1, group_rows), 1))

    def tables(w, carry):
        row = lax.broadcasted_iota(jnp.int32, (rows, LANES), 0) + w * rows
        start = sum(jnp.where(row >= e, c, 0) for e, c in zip(ends, lengths))
        angle = (row - start).astype(jnp.float32) * freq_ref[...]
        cos_t[w] = jnp.cos(angle)
        sine = jnp.sin(angle)
        sin_t[w] = jnp.where(low, -sine, sine)
        seg_j = segments(lax.broadcasted_iota(jnp.int32, (rows, 1), 0) + w * rows)
        bias[w] = jnp.where(seg_j == seg_i, 0.0, -1e30)
        return carry

    lax.fori_loop(0, n, tables, 0)

    for w in others:
        stat_copy(w, w).wait_recv()
    for w in range(n):
        for s in range(2):
            stat[s, :, w * rows:(w + 1) * rows] = stat_in[w, s]

    head_of = lax.broadcasted_iota(jnp.int32, (1, LANES), 1) // head_dim

    def step(p, carry):
        @pl.when(p < chunks - 1)
        def _():
            for w in others:
                in_copy(p, w, me).wait_send()
                in_copy(p + 1, w, me).start()

        in_buf[p, me] = stage[p, me]
        for w in others:
            in_copy(p, w, w).wait_recv()

        def rope(w, c):
            cosv, sinv = cos_t[w], sin_t[w]
            at = pl.ds(pl.multiple_of(w * rows, rows), rows)
            for t, out in ((0, qs), (1, kr)):
                x = in_buf[p, w, t].astype(jnp.float32)
                y = (x * cosv + swap_halves(x, low, half) * sinv).astype(jnp.bfloat16)
                out[at, :] = y * 0.125 if t == 0 else y
            return c

        lax.fori_loop(0, n, rope, 0)
        dq[...] = jnp.zeros_like(dq)

        def keys(w, c):
            k_blk = kr[pl.ds(pl.multiple_of(w * rows, rows), rows), :]
            v_blk = in_buf[p, w, 2]
            q_all = qs[...]
            d_all = in_buf[p, :, 3].reshape(group_rows, LANES)
            gv = jnp.zeros((rows, LANES), jnp.float32)
            gk = jnp.zeros((rows, LANES), jnp.float32)
            ds_list, k_list = [], []
            for a in range(per_chunk):
                mine = head_of == a
                q_a = jnp.where(mine, q_all, 0)
                d_a = jnp.where(mine, d_all, 0)
                k_list.append(jnp.where(mine, k_blk, 0))
                h = pl.ds(p * per_chunk + a, 1)
                s = lax.dot_general(k_blk, q_a, NT, preferred_element_type=jnp.float32)
                prob = jnp.exp(s + bias[w] - stat[0, h, :])
                dp = lax.dot_general(v_blk, d_a, NT, preferred_element_type=jnp.float32)
                ds = (prob * (dp - stat[1, h, :])).astype(jnp.bfloat16)
                gv += jnp.dot(prob.astype(jnp.bfloat16), d_a, preferred_element_type=jnp.float32)
                gk += jnp.dot(ds, q_a, preferred_element_type=jnp.float32)
                ds_list.append(ds)
            ds_all = jnp.concatenate(ds_list, axis=0)
            k_all = jnp.concatenate(k_list, axis=0)
            dq[...] += lax.dot_general(ds_all, k_all, TN, preferred_element_type=jnp.float32)
            grads[p, w, 1] = (gk * cos_t[w] - swap_halves(gk, low, half) * sin_t[w]).astype(jnp.bfloat16)
            grads[p, w, 2] = gv.astype(jnp.bfloat16)
            return c

        lax.fori_loop(0, n, keys, 0)

        def finish(w, c):
            x = dq[pl.ds(pl.multiple_of(w * rows, rows), rows), :] * 0.125
            grads[p, w, 0] = (x * cos_t[w] - swap_halves(x, low, half) * sin_t[w]).astype(jnp.bfloat16)
            return c

        lax.fori_loop(0, n, finish, 0)
        for w in others:
            y_copy(p, w, me).start()
        home[me * chunks + p] = grads[p, me]
        x_copy(me * chunks + p).start()

        for lag, act, sources in events:
            @pl.when(p >= lag)
            def _(lag=lag, act=act, sources=sources):
                act(p - lag, sources)

        return carry

    def pass_on(p, sources):
        for w in sources:
            y_copy(p, w, w).wait_recv()
            x_copy(w * chunks + p).start()

    def pass_relay(p, sources):
        for w in sources:
            b = w * chunks + p
            x_copy(b).wait_recv()

            @pl.when(has_to)
            def _():
                z_copy(b).start()

    events = (
        (0, pass_on, [near_w]),
        (1, pass_on, far),
        (1, pass_relay, [me, near_w]),
        (2, pass_relay, far),
    )

    def drain(p):
        for lag, act, sources in events:
            if 0 <= p - lag < chunks:
                act(p - lag, sources)

    @pl.when(jnp.logical_not(has_from))
    def _():
        relay[...] = jnp.zeros_like(relay)

    lax.fori_loop(0, chunks, step, 0)
    drain(chunks)

    offset = jnp.full((rows, LANES), plan_ref[0, me], jnp.int32)
    toward = jnp.where(even, 1, -1)
    stay, near = offset == 0, offset == toward

    def deliver(b):
        @pl.when(has_from)
        def _():
            z_copy(b).wait_recv()

        at = pl.ds(pl.multiple_of(b * LANES, LANES), LANES)
        for t, out in enumerate((oq_ref, ok_ref, ov_ref)):
            out[:, at] = jnp.where(stay, home[b, t], jnp.where(near, pair[b, t], relay[b, t]))

    def deliver_near(p, c):
        for w in (me, near_w):
            deliver(w * chunks + p)
        return c

    def deliver_far(p, c):
        for w in far:
            deliver(w * chunks + p)
        return c

    lax.fori_loop(0, chunks, deliver_near, 0)
    drain(chunks + 1)
    lax.fori_loop(0, chunks, deliver_far, 0)

    for p in range(chunks):
        for w in others:
            y_copy(p, w, me).wait_send()
    for w in others:
        in_copy(chunks - 1, w, me).wait_send()
        stat_copy(w, me).wait_send()

    def sent(b, c):
        x_copy(b).wait_send()

        @pl.when(has_to)
        def _():
            z_copy(b).wait_send()

        return c

    lax.fori_loop(0, blocks, sent, 0)


def per_device(n, groups, query_in, key_in, value_in, grad_out, fwd_out, log_norm, sample_len, plan_offset):
    rows, cols = query_in.shape
    heads_all = log_norm.shape[1]
    head_dim = cols // heads_all
    half = head_dim // 2
    chunks = cols // n // LANES
    heads = heads_all // n
    group_rows = n * rows
    blocks = n * chunks
    freq = np.power(10000.0, -np.arange(half) / half).astype(np.float32)
    freq = jnp.asarray(np.tile(freq, LANES // half)[None, :])
    bf16, f32 = jnp.bfloat16, jnp.float32
    vmem = pl.BlockSpec(memory_space=pltpu.VMEM)
    smem = pl.BlockSpec(memory_space=pltpu.SMEM)
    hbm = pl.BlockSpec(memory_space=pl.ANY)
    dma = pltpu.SemaphoreType.DMA
    return pl.pallas_call(
        functools.partial(kernel, n, groups, head_dim),
        out_shape=(pltpu.VMEM((rows, cols), bf16),) * 3,
        in_specs=[vmem, smem, smem, vmem, hbm, hbm, hbm, hbm, hbm],
        out_specs=(vmem, vmem, vmem),
        scratch_shapes=[
            pltpu.VMEM((chunks, n, 4, rows, LANES), bf16),
            pltpu.VMEM((chunks, n, 4, rows, LANES), bf16),
            pltpu.VMEM((rows, cols), bf16),
            pltpu.VMEM((n, 2, heads, rows), f32),
            pltpu.VMEM((n, 2, heads, rows), f32),
            pltpu.VMEM((2, heads, group_rows), f32),
            pltpu.VMEM((n, rows, LANES), f32),
            pltpu.VMEM((n, rows, LANES), f32),
            pltpu.VMEM((n, rows, group_rows), f32),
            pltpu.VMEM((group_rows, LANES), bf16),
            pltpu.VMEM((group_rows, LANES), bf16),
            pltpu.VMEM((group_rows, LANES), f32),
            pltpu.VMEM((chunks, n, 3, rows, LANES), bf16),
            pltpu.VMEM((blocks, 3, rows, LANES), bf16),
            pltpu.VMEM((blocks, 3, rows, LANES), bf16),
            pltpu.VMEM((blocks, 3, rows, LANES), bf16),
            dma((chunks, n)),
            dma((chunks, n)),
            dma((n,)),
            dma((n,)),
            dma((chunks, n)),
            dma((chunks, n)),
            dma((blocks,)),
            dma((blocks,)),
            dma((blocks,)),
            dma((blocks,)),
            dma((chunks, 4, n)),
            dma,
        ],
        compiler_params=pltpu.CompilerParams(collective_id=0, has_side_effects=True),
    )(freq, sample_len, plan_offset, log_norm.T, query_in, key_in, value_in, grad_out, fwd_out)


CORES = 2
LAG = 2
INPUTS = 4
GRADS = 3


def spread(x, slots, half):
    groups = LANES // half
    turned = [x] + [pltpu.roll(x, half * j, 1) for j in range(1, groups)]
    group = lax.broadcasted_iota(jnp.int32, x.shape, 1) // half
    out = []
    for s in range(slots):
        y = turned[(groups - 1 - s) % groups]
        for j in range(groups - 1):
            y = jnp.where(group == j, turned[(j - s) % groups], y)
        out.append(y)
    return out


def halves_kernel(
    groups, head_dim, lag,
    freq_ref, len_ref, plan_ref, lse_ref, q_ref, k_ref, v_ref, d_ref, f_ref,
    oq_ref, ok_ref, ov_ref,
    in_buf, stage, f_vm, y_in, y_out, stat_oth, stat_in, stat, cos_t, sin_t, bias,
    qs, kr, dd, dsb, km, acc, grad, keep, home, pair, relay,
    l_sem, f_sem, c_send, c_recv, st_send, st_recv, d_send, y_send, y_recv,
    x_send, x_recv, h_send, h_recv, z_send, z_recv,
):
    f32, bf16 = jnp.float32, jnp.bfloat16
    g = lax.axis_index("grp")
    me = lax.axis_index("ulys")
    heads_all, rows = lse_ref.shape
    heads = heads_all // CORES
    chunks = in_buf.shape[0]
    width = chunks * LANES
    per_chunk = LANES // head_dim
    half = head_dim // 2
    slots = CORES + 1
    span = slots * rows
    inputs = (q_ref, k_ref, v_ref, d_ref)

    c = lax.rem(me, CORES)
    yc = me // CORES
    far, near = yc, 1 - yc
    sib = me + 1 - 2 * c
    opp_base = CORES * (1 - yc)
    mate_base = CORES * yc
    is_near, is_far = c == near, c == far

    even = lax.rem(g, 2) == 0
    partner = jnp.where(even, g + 1, g - 1)
    up, down = g + 2, g - 2
    has_up, has_down = up < groups, down >= 0
    z_to = jnp.where(even, up, down)
    has_to = jnp.where(even, has_up, has_down)
    has_from = jnp.where(even, has_down, has_up)

    barrier = pltpu.get_barrier_semaphore()
    peers = [(g, sib)] + [(g, opp_base + o) for o in range(CORES)]
    peers += [(partner, mate_base + o) for o in range(CORES)]
    for peer in peers:
        pl.semaphore_signal(barrier, inc=1, device_id=peer, device_id_type=MESH)

    @pl.when(has_up)
    def _():
        pl.semaphore_signal(barrier, inc=1, device_id=(up, me), device_id_type=MESH)

    @pl.when(has_down)
    def _():
        pl.semaphore_signal(barrier, inc=1, device_id=(down, me), device_id_type=MESH)

    def load(p, t, other):
        w = 1 - c if other else c
        dst = stage.at[p, t] if other else in_buf.at[p, c, t]
        return pltpu.make_async_copy(
            inputs[t].at[:, pl.ds(pl.multiple_of(w * width + p * LANES, LANES), LANES)],
            dst, l_sem.at[p, t, int(other)],
        )

    def load_f(other):
        w = 1 - c if other else c
        return pltpu.make_async_copy(
            f_ref.at[:, pl.ds(pl.multiple_of(w * width, LANES), width)], f_vm.at[int(other)], f_sem.at[int(other)],
        )

    def remote(src, dst, send, recv, to):
        return pltpu.make_async_remote_copy(
            src_ref=src, dst_ref=dst, send_sem=send, recv_sem=recv, device_id=to, device_id_type=MESH,
        )

    def core_copy(p, slot):
        return remote(stage.at[p], in_buf.at[p, slot], c_send.at[p], c_recv.at[p], (g, sib))

    def first_copy(m, other):
        src = stage.at[m] if other else in_buf.at[m, c]
        to = 1 - c if other else c
        return remote(src, y_in.at[m], d_send.at[m, int(other)], y_recv.at[m], (g, opp_base + to))

    def y_copy(p):
        return remote(y_out.at[p], y_in.at[p + lag], y_send.at[p], y_recv.at[p + lag], (g, opp_base + c))

    def y_arrival(m):
        return remote(y_out.at[0], y_in.at[m], y_send.at[0], y_recv.at[m], (g, opp_base + c))

    def y_last_arrival(m):
        keep_to = pl.ds(0, GRADS)
        return remote(
            y_out.at[0, keep_to], y_in.at[m, keep_to], y_send.at[0], y_recv.at[m], (g, opp_base + c)
        )

    def y_last(p):
        return remote(
            y_out.at[p, pl.ds(0, GRADS)], y_in.at[p + lag, pl.ds(0, GRADS)],
            y_send.at[p], y_recv.at[p + lag], (g, opp_base + c),
        )

    def stat_core(slot):
        return remote(stat_oth, stat_in.at[slot], st_send.at[0], st_recv.at[slot], (g, sib))

    def stat_far(other):
        src = stat_oth if other else stat_in.at[c]
        to = 1 - c if other else c
        return remote(src, stat_in.at[CORES], st_send.at[1 + int(other)], st_recv.at[CORES], (g, opp_base + to))

    def x_copy(p, slot, kind, h):
        return remote(
            grad.at[p, slot], pair.at[h, p], x_send.at[kind, p], x_recv.at[h, p], (partner, mate_base + slot),
        )

    def home_copy(p, h):
        return remote(grad.at[p, 1 - c], home.at[h, p], h_send.at[p], h_recv.at[p], (g, sib))

    def z_copy(h, p):
        return remote(pair.at[h, p], relay.at[h, p], z_send.at[h, p], z_recv.at[h, p], (z_to, me))

    for t in range(INPUTS):
        for other in (False, True):
            load(0, t, other).start()
    load_f(False).start()
    load_f(True).start()
    for p in range(1, chunks):
        for t in reversed(range(INPUTS)):
            for other in (False, True):
                load(p, t, other).start()

    lengths = [len_ref[0, s] for s in range(len_ref.shape[1])]
    ends = []
    for s, length in enumerate(lengths):
        ends.append(length if s == 0 else ends[-1] + length)
    cut = sum(jnp.where(e <= CORES * rows, n, 0) for e, n in zip(ends, lengths))
    ship = jnp.where(cut >= rows, 1 - yc, yc)
    lane = lax.broadcasted_iota(jnp.int32, (rows, LANES), 1)
    low = lax.rem(lane, head_dim) < half
    shipping = jnp.full((rows, LANES), ship, jnp.int32) == 1

    def segments(index):
        return sum((index >= e).astype(jnp.int32) for e in ends)

    other_at = (2 - yc) * rows
    own_at = mate_base * rows
    group = lane // half
    row = lax.broadcasted_iota(jnp.int32, (rows, LANES), 0)
    row = jnp.where(group < CORES, own_at + group * rows, other_at) + row
    start = sum(jnp.where(row >= e, n, 0) for e, n in zip(ends, lengths))
    angle = (row - start).astype(f32) * freq_ref[...]
    for s, value in enumerate(spread(jnp.cos(angle), slots, half)):
        cos_t[s] = value
    for s, value in enumerate(spread(jnp.sin(angle), slots, half)):
        sin_t[s] = jnp.where(low, -value, value)

    col = lax.broadcasted_iota(jnp.int32, (1, span), 1)
    own_col = col < CORES * rows
    seg_i = segments(jnp.where(own_col, own_at + col, other_at - CORES * rows + col))
    sent = jnp.full((1, span), ship, jnp.int32) == 1
    for s in range(slots):
        at = own_at + s * rows if s < CORES else other_at
        seg_j = segments(lax.broadcasted_iota(jnp.int32, (rows, 1), 0) + at)
        if s < CORES:
            same = seg_j == jnp.where(own_col, seg_i, jnp.where(sent, -1, seg_i))
        else:
            same = seg_j == jnp.where(own_col, jnp.where(sent, -1, seg_i), -1)
        bias[s] = jnp.where(same, 0.0, -1e30)

    for t in range(INPUTS):
        for other in (False, True):
            load(0, t, other).wait()
    pl.semaphore_wait(barrier, len(peers) + has_up.astype(jnp.int32) + has_down.astype(jnp.int32))

    @pl.when(is_near)
    def _():
        first_copy(0, False).start()
        first_copy(0, True).start()

    core_copy(0, c).start()

    for p in range(1, chunks):
        for other in (False, True):
            load(p, INPUTS - 1, other).wait()
    for other in (False, True):
        load_f(other).wait()
    owner = lax.broadcasted_iota(jnp.int32, (heads, width), 1) - head_dim * lax.broadcasted_iota(
        jnp.int32, (heads, width), 0
    )
    pick = jnp.where((owner >= 0) & (owner < head_dim), 1.0, 0.0).astype(bf16)
    for other in (True, False):
        if other:
            tiles = [stage[p, INPUTS - 1] for p in range(chunks)]
        else:
            tiles = [in_buf[p, c, INPUTS - 1] for p in range(chunks)]
        prod = jnp.concatenate(tiles, axis=1).astype(f32) * f_vm[int(other)].astype(f32)
        high = prod.astype(bf16)
        rest = (prod - high.astype(f32)).astype(bf16)
        delta = lax.dot_general(pick, high, NT, preferred_element_type=f32)
        delta += lax.dot_general(pick, rest, NT, preferred_element_type=f32)
        w = 1 - c if other else c
        lse = lse_ref[pl.ds(pl.multiple_of(w * heads, heads), heads), :]
        if other:
            stat_oth[0] = lse
            stat_oth[1] = delta
        else:
            stat_in[c, 0] = lse
            stat_in[c, 1] = delta
    stat_core(c).start()

    @pl.when(is_near)
    def _():
        stat_far(False).start()
        stat_far(True).start()

    for p in range(1, chunks):
        for t in range(INPUTS - 1):
            for other in (False, True):
                load(p, t, other).wait()
        if p < lag:
            @pl.when(is_near)
            def _(p=p):
                first_copy(p, False).start()
                first_copy(p, True).start()

        core_copy(p, c).start()

    @pl.when(jnp.logical_not(has_from))
    def _():
        relay[...] = jnp.zeros_like(relay)

    stat_core(1 - c).wait_recv()
    stat_far(False).wait_recv()
    for s in range(slots):
        stat[:, :, s * rows:(s + 1) * rows] = stat_in[s]
    for p in range(min(lag, chunks)):
        core_copy(p, 1 - c).wait_recv()

    head_of = lax.broadcasted_iota(jnp.int32, (1, LANES), 1) // head_dim

    def turn_back(x, s):
        return x * cos_t[s] - swap_halves(x, low, half) * sin_t[s]

    def compute(p):
        for s in range(slots):
            at = slice(s * rows, (s + 1) * rows)

            def take(t):
                return in_buf[p, s, t] if s < CORES else y_in[p, t]

            for t, out in ((0, qs), (1, kr)):
                x = take(t).astype(f32)
                y = (x * cos_t[s] + swap_halves(x, low, half) * sin_t[s]).astype(bf16)
                out[at, :] = y * 0.125 if t == 0 else y
            dd[at, :] = take(3)
        shares = []
        for s in range(slots):
            k_blk = kr[s * rows:(s + 1) * rows, :]
            v_blk = in_buf[p, s, 2] if s < CORES else y_in[p, 2]
            q_all, d_all = qs[...], dd[...]
            gv = jnp.zeros((rows, LANES), f32)
            gk = jnp.zeros((rows, LANES), f32)
            for a in range(per_chunk):
                mine = head_of == a
                q_a = jnp.where(mine, q_all, 0)
                d_a = jnp.where(mine, d_all, 0)
                at = slice((s * per_chunk + a) * rows, (s * per_chunk + a + 1) * rows)
                km[at, :] = jnp.where(mine, k_blk, 0)
                h = pl.ds(p * per_chunk + a, 1)
                score = lax.dot_general(k_blk, q_a, NT, preferred_element_type=f32)
                prob = jnp.exp(score + bias[s] - stat[0, h, :])
                dp = lax.dot_general(v_blk, d_a, NT, preferred_element_type=f32)
                ds = (prob * (dp - stat[1, h, :])).astype(bf16)
                gv += jnp.dot(prob.astype(bf16), d_a, preferred_element_type=f32)
                gk += jnp.dot(ds, q_a, preferred_element_type=f32)
                dsb[at, :] = ds
            gk = turn_back(gk, s)
            if s < CORES:
                acc[s, 1] = gk
                acc[s, 2] = gv
            else:
                shares = [gk, gv]
        dq = lax.dot_general(dsb[...], km[...], TN, preferred_element_type=f32) * 0.125
        for s in range(slots):
            part = turn_back(dq[s * rows:(s + 1) * rows, :], s)
            if s < CORES:
                acc[s, 0] = part
            else:
                shares = [part] + shares
        m = jnp.minimum(p + lag, chunks - 1)
        for t in range(GRADS):
            y_out[p, t] = jnp.where(shipping, in_buf[m, near, t], shares[t].astype(bf16))
        y_out[p, 3] = in_buf[m, near, 3]

        @pl.when(p + lag < chunks)
        def _():
            y_copy(p).start()

        @pl.when(p + lag >= chunks)
        def _():
            y_last(p).start()

        for t in range(GRADS):
            grad[p, far, t] = acc[far, t].astype(bf16)
            keep[p, t] = acc[near, t]

    def hand_on(p, slot, kind):
        x_copy(p, slot, kind, c).start()

        @pl.when(c == slot)
        def _():
            home[c, p] = grad[p, slot]

        @pl.when(c != slot)
        def _():
            home_copy(p, c).start()

    offset = jnp.full((rows, LANES), plan_ref[0, me], jnp.int32)
    toward = jnp.where(even, 1, -1)
    stay, beside = offset == 0, offset == toward
    wait_x = jnp.where(is_far, 1, lag + 1)

    def deliver(q):
        home_copy(q, 1 - c).wait_recv()
        for h in range(CORES):
            @pl.when(has_from)
            def _(h=h):
                z_copy(h, q).wait_recv()

            at = pl.ds(pl.multiple_of((h * chunks + q) * LANES, LANES), LANES)
            for t, out in enumerate((oq_ref, ok_ref, ov_ref)):
                out[:, at] = jnp.where(stay, home[h, q, t], jnp.where(beside, pair[h, q, t], relay[h, q, t]))

    def step(p, carry):
        @pl.when(p + lag < chunks)
        def _():
            core_copy(p + lag, 1 - c).wait_recv()

        @pl.when(p < chunks)
        def _():
            y_arrival(p).wait_recv()

        @pl.when((p >= chunks) & (p < chunks + lag))
        def _():
            y_last_arrival(p).wait_recv()

        @pl.when((p >= lag) & (p < chunks + lag))
        def _():
            q = p - lag
            for t in range(GRADS):
                got = jnp.where(shipping, y_in[p, t].astype(f32), 0.0)
                grad[q, near, t] = (keep[q, t] + got).astype(bf16)
            hand_on(q, near, 1)

        @pl.when(p < chunks)
        def _():
            compute(p)
            hand_on(p, far, 0)

        at = p - wait_x

        @pl.when((at >= 0) & (at < chunks))
        def _():
            for h in range(CORES):
                x_copy(at, c, 0, h).wait_recv()

                @pl.when(has_to)
                def _(h=h):
                    z_copy(h, at).start()

        done = at - 2

        @pl.when((done >= 0) & (done < chunks))
        def _():
            deliver(done)

        return carry

    lax.fori_loop(0, chunks + lag + 3, step, 0)

    stat_core(c).wait_send()

    @pl.when(is_near)
    def _():
        for other in (False, True):
            stat_far(other).wait_send()
            for m in range(lag):
                first_copy(m, other).wait_send()

    def drain(p, carry):
        core_copy(p, c).wait_send()

        @pl.when(p + lag < chunks)
        def _():
            y_copy(p).wait_send()

        @pl.when(p + lag >= chunks)
        def _():
            y_last(p).wait_send()

        x_copy(p, far, 0, c).wait_send()
        x_copy(p, near, 1, c).wait_send()
        home_copy(p, c).wait_send()

        @pl.when(has_to)
        def _():
            for h in range(CORES):
                z_copy(h, p).wait_send()

        return carry

    lax.fori_loop(0, chunks, drain, 0)


def per_device_halves(n, groups, query_in, key_in, value_in, grad_out, fwd_out, log_norm, sample_len, plan_offset):
    rows, cols = query_in.shape
    heads_all = log_norm.shape[1]
    head_dim = cols // heads_all
    half = head_dim // 2
    chunks = cols // CORES // LANES
    heads = heads_all // CORES
    slots = CORES + 1
    per_chunk = LANES // head_dim
    lag = min(LAG, chunks)
    freq = np.power(10000.0, -np.arange(half) / half).astype(np.float32)
    freq = jnp.asarray(np.tile(freq, LANES // half)[None, :])
    bf16, f32 = jnp.bfloat16, jnp.float32
    vmem = pl.BlockSpec(memory_space=pltpu.VMEM)
    smem = pl.BlockSpec(memory_space=pltpu.SMEM)
    hbm = pl.BlockSpec(memory_space=pl.ANY)
    dma = pltpu.SemaphoreType.DMA
    return pl.pallas_call(
        functools.partial(halves_kernel, groups, head_dim, lag),
        out_shape=(pltpu.VMEM((rows, cols), bf16),) * 3,
        in_specs=[vmem, smem, smem, vmem, hbm, hbm, hbm, hbm, hbm],
        out_specs=(vmem, vmem, vmem),
        scratch_shapes=[
            pltpu.VMEM((chunks, CORES, INPUTS, rows, LANES), bf16),
            pltpu.VMEM((chunks, INPUTS, rows, LANES), bf16),
            pltpu.VMEM((CORES, rows, cols // CORES), bf16),
            pltpu.VMEM((chunks + lag, INPUTS, rows, LANES), bf16),
            pltpu.VMEM((chunks, INPUTS, rows, LANES), bf16),
            pltpu.VMEM((2, heads, rows), f32),
            pltpu.VMEM((slots, 2, heads, rows), f32),
            pltpu.VMEM((2, heads, slots * rows), f32),
            pltpu.VMEM((slots, rows, LANES), f32),
            pltpu.VMEM((slots, rows, LANES), f32),
            pltpu.VMEM((slots, rows, slots * rows), f32),
            pltpu.VMEM((slots * rows, LANES), bf16),
            pltpu.VMEM((slots * rows, LANES), bf16),
            pltpu.VMEM((slots * rows, LANES), bf16),
            pltpu.VMEM((slots * per_chunk * rows, slots * rows), bf16),
            pltpu.VMEM((slots * per_chunk * rows, LANES), bf16),
            pltpu.VMEM((CORES, GRADS, rows, LANES), f32),
            pltpu.VMEM((chunks, CORES, GRADS, rows, LANES), bf16),
            pltpu.VMEM((chunks, GRADS, rows, LANES), f32),
            pltpu.VMEM((CORES, chunks, GRADS, rows, LANES), bf16),
            pltpu.VMEM((CORES, chunks, GRADS, rows, LANES), bf16),
            pltpu.VMEM((CORES, chunks, GRADS, rows, LANES), bf16),
            dma((chunks, INPUTS, 2)),
            dma((2,)),
            dma((chunks,)),
            dma((chunks,)),
            dma((3,)),
            dma((slots,)),
            dma((lag, 2)),
            dma((chunks,)),
            dma((chunks + lag,)),
            dma((2, chunks)),
            dma((CORES, chunks)),
            dma((chunks,)),
            dma((chunks,)),
            dma((CORES, chunks)),
            dma((CORES, chunks)),
        ],
        compiler_params=pltpu.CompilerParams(collective_id=0, has_side_effects=True),
    )(freq, sample_len, plan_offset, log_norm.T, query_in, key_in, value_in, grad_out, fwd_out)


def solution(mesh):
    tokens = P(("grp", "ulys"), None)
    in_specs = (tokens,) * 6 + (P("grp", None), P("grp", None))
    n = mesh.shape["ulys"]
    two_chips = n == 2 * CORES
    body = functools.partial(per_device_halves if two_chips else per_device, n, mesh.shape["grp"])
    return jax.shard_map(
        body, mesh=mesh, in_specs=in_specs, out_specs=(tokens,) * 3, check_vma=False
    )
```

```python
import functools

import jax
import jax.numpy as jnp
import numpy as np
from jax import lax
from jax.experimental import pallas as pl
from jax.experimental.pallas import tpu as pltpu
from jax.sharding import PartitionSpec as P

MESH = pl.DeviceIdType.MESH
LANES = 128
NT = (((1,), (1,)), ((), ()))
TN = (((0,), (0,)), ((), ()))


def swap_halves(x, low, half):
    return jnp.where(low, pltpu.roll(x, LANES - half, 1), pltpu.roll(x, half, 1))


def kernel(
    n, groups, head_dim,
    freq_ref, len_ref, plan_ref, lse_ref, q_ref, k_ref, v_ref, d_ref, f_ref,
    oq_ref, ok_ref, ov_ref,
    stage, in_buf, f_vm, stat_out, stat_in, stat, cos_t, sin_t, bias,
    qs, kr, dq, grads, home, pair, relay,
    in_send, in_recv, st_send, st_recv, y_send, y_recv, x_send, x_recv, z_send, z_recv,
    loc_sem, df_sem,
):
    g = lax.axis_index("grp")
    me = lax.axis_index("ulys")
    heads_all, rows = lse_ref.shape
    heads = heads_all // n
    chunks = in_buf.shape[0]
    width = chunks * LANES
    per_chunk = LANES // head_dim
    half = head_dim // 2
    group_rows = n * rows
    blocks = n * chunks
    inputs = (q_ref, k_ref, v_ref, d_ref)

    even = lax.rem(g, 2) == 0
    partner = jnp.where(even, g + 1, g - 1)
    up, down = g + 2, g - 2
    has_up, has_down = up < groups, down >= 0
    z_to = jnp.where(even, up, down)
    has_to = jnp.where(even, up < groups, down >= 0)
    has_from = jnp.where(even, down >= 0, up < groups)

    barrier = pltpu.get_barrier_semaphore()
    near_w = jnp.where(lax.rem(me, 2) == 0, me + 1, me - 1)
    far = [lax.rem(near_w - lax.rem(near_w, 2) + o, n) for o in range(2, n)]
    others = far + [near_w]
    for w in others:
        pl.semaphore_signal(barrier, inc=1, device_id=(g, w), device_id_type=MESH)
    pl.semaphore_signal(barrier, inc=1, device_id=(partner, me), device_id_type=MESH)

    @pl.when(has_up)
    def _():
        pl.semaphore_signal(barrier, inc=1, device_id=(up, me), device_id_type=MESH)

    @pl.when(has_down)
    def _():
        pl.semaphore_signal(barrier, inc=1, device_id=(down, me), device_id_type=MESH)

    def load(p, t, w):
        return pltpu.make_async_copy(
            inputs[t].at[:, pl.ds(pl.multiple_of(w * width + p * LANES, LANES), LANES)],
            stage.at[p, w, t],
            loc_sem.at[p, t, w],
        )

    for p in range(chunks):
        for w in far + [near_w, me]:
            for t in range(4):
                load(p, t, w).start()
    copy_f = pltpu.make_async_copy(f_ref, f_vm, df_sem)
    copy_f.start()

    pl.semaphore_wait(barrier, n + has_up.astype(jnp.int32) + has_down.astype(jnp.int32))

    def in_copy(p, w, src):
        return pltpu.make_async_remote_copy(
            src_ref=stage.at[p, w],
            dst_ref=in_buf.at[p, src],
            send_sem=in_send.at[p, w],
            recv_sem=in_recv.at[p, src],
            device_id=(g, w),
            device_id_type=MESH,
        )

    def stat_copy(w, src):
        return pltpu.make_async_remote_copy(
            src_ref=stat_out.at[w], dst_ref=stat_in.at[src],
            send_sem=st_send.at[w], recv_sem=st_recv.at[src],
            device_id=(g, w), device_id_type=MESH,
        )

    def y_copy(p, w, src):
        return pltpu.make_async_remote_copy(
            src_ref=grads.at[p, w], dst_ref=home.at[src * chunks + p],
            send_sem=y_send.at[p, w], recv_sem=y_recv.at[p, src],
            device_id=(g, w), device_id_type=MESH,
        )

    def x_copy(b):
        return pltpu.make_async_remote_copy(
            src_ref=home.at[b], dst_ref=pair.at[b],
            send_sem=x_send.at[b], recv_sem=x_recv.at[b],
            device_id=(partner, me), device_id_type=MESH,
        )

    def z_copy(b):
        return pltpu.make_async_remote_copy(
            src_ref=pair.at[b], dst_ref=relay.at[b],
            send_sem=z_send.at[b], recv_sem=z_recv.at[b],
            device_id=(z_to, me), device_id_type=MESH,
        )

    for p in range(chunks):
        for w in others:
            for t in range(4):
                load(p, t, w).wait()
            if p == 0:
                in_copy(p, w, me).start()
        for t in range(4):
            load(p, t, me).wait()

    copy_f.wait()
    cols = f_vm.shape[1]
    d_full = jnp.concatenate([stage[p, w, 3] for w in range(n) for p in range(chunks)], axis=1)
    prod = d_full.astype(jnp.float32) * f_vm[...].astype(jnp.float32)
    high = prod.astype(jnp.bfloat16)
    rest = (prod - high.astype(jnp.float32)).astype(jnp.bfloat16)
    owner = lax.broadcasted_iota(jnp.int32, (heads_all, cols), 1) - head_dim * lax.broadcasted_iota(
        jnp.int32, (heads_all, cols), 0
    )
    pick = jnp.where((owner >= 0) & (owner < head_dim), 1.0, 0.0).astype(jnp.bfloat16)
    delta = lax.dot_general(pick, high, NT, preferred_element_type=jnp.float32)
    delta += lax.dot_general(pick, rest, NT, preferred_element_type=jnp.float32)
    lse = lse_ref[...]
    for w in range(n):
        stat_out[w, 0] = lse[w * heads:(w + 1) * heads]
        stat_out[w, 1] = delta[w * heads:(w + 1) * heads]
    for w in others:
        stat_copy(w, me).start()
    stat_in[me] = stat_out[me]

    lengths = [len_ref[0, s] for s in range(len_ref.shape[1])]
    ends = []
    for s, length in enumerate(lengths):
        ends.append(length if s == 0 else ends[-1] + length)
    lane = lax.broadcasted_iota(jnp.int32, (rows, LANES), 1)
    low = lax.rem(lane, head_dim) < half

    def segments(index):
        return sum((index >= e).astype(jnp.int32) for e in ends)

    seg_i = segments(lax.broadcasted_iota(jnp.int32, (1, group_rows), 1))

    def tables(w, carry):
        row = lax.broadcasted_iota(jnp.int32, (rows, LANES), 0) + w * rows
        start = sum(jnp.where(row >= e, c, 0) for e, c in zip(ends, lengths))
        angle = (row - start).astype(jnp.float32) * freq_ref[...]
        cos_t[w] = jnp.cos(angle)
        sine = jnp.sin(angle)
        sin_t[w] = jnp.where(low, -sine, sine)
        seg_j = segments(lax.broadcasted_iota(jnp.int32, (rows, 1), 0) + w * rows)
        bias[w] = jnp.where(seg_j == seg_i, 0.0, -1e30)
        return carry

    lax.fori_loop(0, n, tables, 0)

    for w in others:
        stat_copy(w, w).wait_recv()
    for w in range(n):
        for s in range(2):
            stat[s, :, w * rows:(w + 1) * rows] = stat_in[w, s]

    head_of = lax.broadcasted_iota(jnp.int32, (1, LANES), 1) // head_dim

    def step(p, carry):
        @pl.when(p < chunks - 1)
        def _():
            for w in others:
                in_copy(p, w, me).wait_send()
                in_copy(p + 1, w, me).start()

        in_buf[p, me] = stage[p, me]
        for w in others:
            in_copy(p, w, w).wait_recv()

        def rope(w, c):
            cosv, sinv = cos_t[w], sin_t[w]
            at = pl.ds(pl.multiple_of(w * rows, rows), rows)
            for t, out in ((0, qs), (1, kr)):
                x = in_buf[p, w, t].astype(jnp.float32)
                y = (x * cosv + swap_halves(x, low, half) * sinv).astype(jnp.bfloat16)
                out[at, :] = y * 0.125 if t == 0 else y
            return c

        lax.fori_loop(0, n, rope, 0)
        dq[...] = jnp.zeros_like(dq)

        def keys(w, c):
            k_blk = kr[pl.ds(pl.multiple_of(w * rows, rows), rows), :]
            v_blk = in_buf[p, w, 2]
            q_all = qs[...]
            d_all = in_buf[p, :, 3].reshape(group_rows, LANES)
            gv = jnp.zeros((rows, LANES), jnp.float32)
            gk = jnp.zeros((rows, LANES), jnp.float32)
            ds_list, k_list = [], []
            for a in range(per_chunk):
                mine = head_of == a
                q_a = jnp.where(mine, q_all, 0)
                d_a = jnp.where(mine, d_all, 0)
                k_list.append(jnp.where(mine, k_blk, 0))
                h = pl.ds(p * per_chunk + a, 1)
                s = lax.dot_general(k_blk, q_a, NT, preferred_element_type=jnp.float32)
                prob = jnp.exp(s + bias[w] - stat[0, h, :])
                dp = lax.dot_general(v_blk, d_a, NT, preferred_element_type=jnp.float32)
                ds = (prob * (dp - stat[1, h, :])).astype(jnp.bfloat16)
                gv += jnp.dot(prob.astype(jnp.bfloat16), d_a, preferred_element_type=jnp.float32)
                gk += jnp.dot(ds, q_a, preferred_element_type=jnp.float32)
                ds_list.append(ds)
            ds_all = jnp.concatenate(ds_list, axis=0)
            k_all = jnp.concatenate(k_list, axis=0)
            dq[...] += lax.dot_general(ds_all, k_all, TN, preferred_element_type=jnp.float32)
            grads[p, w, 1] = (gk * cos_t[w] - swap_halves(gk, low, half) * sin_t[w]).astype(jnp.bfloat16)
            grads[p, w, 2] = gv.astype(jnp.bfloat16)
            return c

        lax.fori_loop(0, n, keys, 0)

        def finish(w, c):
            x = dq[pl.ds(pl.multiple_of(w * rows, rows), rows), :] * 0.125
            grads[p, w, 0] = (x * cos_t[w] - swap_halves(x, low, half) * sin_t[w]).astype(jnp.bfloat16)
            return c

        lax.fori_loop(0, n, finish, 0)
        for w in others:
            y_copy(p, w, me).start()
        home[me * chunks + p] = grads[p, me]
        x_copy(me * chunks + p).start()

        for lag, act, sources in events:
            @pl.when(p >= lag)
            def _(lag=lag, act=act, sources=sources):
                act(p - lag, sources)

        return carry

    def pass_on(p, sources):
        for w in sources:
            y_copy(p, w, w).wait_recv()
            x_copy(w * chunks + p).start()

    def pass_relay(p, sources):
        for w in sources:
            b = w * chunks + p
            x_copy(b).wait_recv()

            @pl.when(has_to)
            def _():
                z_copy(b).start()

    events = (
        (0, pass_on, [near_w]),
        (1, pass_on, far),
        (1, pass_relay, [me, near_w]),
        (2, pass_relay, far),
    )

    def drain(p):
        for lag, act, sources in events:
            if 0 <= p - lag < chunks:
                act(p - lag, sources)

    @pl.when(jnp.logical_not(has_from))
    def _():
        relay[...] = jnp.zeros_like(relay)

    lax.fori_loop(0, chunks, step, 0)
    drain(chunks)

    offset = jnp.full((rows, LANES), plan_ref[0, me], jnp.int32)
    toward = jnp.where(even, 1, -1)
    stay, near = offset == 0, offset == toward

    def deliver(b):
        @pl.when(has_from)
        def _():
            z_copy(b).wait_recv()

        at = pl.ds(pl.multiple_of(b * LANES, LANES), LANES)
        for t, out in enumerate((oq_ref, ok_ref, ov_ref)):
            out[:, at] = jnp.where(stay, home[b, t], jnp.where(near, pair[b, t], relay[b, t]))

    def deliver_near(p, c):
        for w in (me, near_w):
            deliver(w * chunks + p)
        return c

    def deliver_far(p, c):
        for w in far:
            deliver(w * chunks + p)
        return c

    lax.fori_loop(0, chunks, deliver_near, 0)
    drain(chunks + 1)
    lax.fori_loop(0, chunks, deliver_far, 0)

    for p in range(chunks):
        for w in others:
            y_copy(p, w, me).wait_send()
    for w in others:
        in_copy(chunks - 1, w, me).wait_send()
        stat_copy(w, me).wait_send()

    def sent(b, c):
        x_copy(b).wait_send()

        @pl.when(has_to)
        def _():
            z_copy(b).wait_send()

        return c

    lax.fori_loop(0, blocks, sent, 0)


def per_device(n, groups, query_in, key_in, value_in, grad_out, fwd_out, log_norm, sample_len, plan_offset):
    rows, cols = query_in.shape
    heads_all = log_norm.shape[1]
    head_dim = cols // heads_all
    half = head_dim // 2
    chunks = cols // n // LANES
    heads = heads_all // n
    group_rows = n * rows
    blocks = n * chunks
    freq = np.power(10000.0, -np.arange(half) / half).astype(np.float32)
    freq = jnp.asarray(np.tile(freq, LANES // half)[None, :])
    bf16, f32 = jnp.bfloat16, jnp.float32
    vmem = pl.BlockSpec(memory_space=pltpu.VMEM)
    smem = pl.BlockSpec(memory_space=pltpu.SMEM)
    hbm = pl.BlockSpec(memory_space=pl.ANY)
    dma = pltpu.SemaphoreType.DMA
    return pl.pallas_call(
        functools.partial(kernel, n, groups, head_dim),
        out_shape=(pltpu.VMEM((rows, cols), bf16),) * 3,
        in_specs=[vmem, smem, smem, vmem, hbm, hbm, hbm, hbm, hbm],
        out_specs=(vmem, vmem, vmem),
        scratch_shapes=[
            pltpu.VMEM((chunks, n, 4, rows, LANES), bf16),
            pltpu.VMEM((chunks, n, 4, rows, LANES), bf16),
            pltpu.VMEM((rows, cols), bf16),
            pltpu.VMEM((n, 2, heads, rows), f32),
            pltpu.VMEM((n, 2, heads, rows), f32),
            pltpu.VMEM((2, heads, group_rows), f32),
            pltpu.VMEM((n, rows, LANES), f32),
            pltpu.VMEM((n, rows, LANES), f32),
            pltpu.VMEM((n, rows, group_rows), f32),
            pltpu.VMEM((group_rows, LANES), bf16),
            pltpu.VMEM((group_rows, LANES), bf16),
            pltpu.VMEM((group_rows, LANES), f32),
            pltpu.VMEM((chunks, n, 3, rows, LANES), bf16),
            pltpu.VMEM((blocks, 3, rows, LANES), bf16),
            pltpu.VMEM((blocks, 3, rows, LANES), bf16),
            pltpu.VMEM((blocks, 3, rows, LANES), bf16),
            dma((chunks, n)),
            dma((chunks, n)),
            dma((n,)),
            dma((n,)),
            dma((chunks, n)),
            dma((chunks, n)),
            dma((blocks,)),
            dma((blocks,)),
            dma((blocks,)),
            dma((blocks,)),
            dma((chunks, 4, n)),
            dma,
        ],
        compiler_params=pltpu.CompilerParams(collective_id=0, has_side_effects=True),
    )(freq, sample_len, plan_offset, log_norm.T, query_in, key_in, value_in, grad_out, fwd_out)


CORES = 2
LAG = 2
LATE = 2
RELAY = 2
INPUTS = 4
GRADS = 3


def spread(x, slots, half):
    groups = LANES // half
    turned = [x] + [pltpu.roll(x, half * j, 1) for j in range(1, groups)]
    group = lax.broadcasted_iota(jnp.int32, x.shape, 1) // half
    out = []
    for s in range(slots):
        y = turned[(groups - 1 - s) % groups]
        for j in range(groups - 1):
            y = jnp.where(group == j, turned[(j - s) % groups], y)
        out.append(y)
    return out


def halves_kernel(
    groups, head_dim, lag, early,
    freq_hbm, len_hbm, plan_hbm, lse_hbm, q_ref, k_ref, v_ref, d_ref, f_ref,
    oq_ref, ok_ref, ov_ref,
    freq_ref, len_ref, plan_ref, lse_ref, in_buf, stage, f_vm, y_in, y_out, stat_oth, stat_in, stat, cos_t, sin_t, bias,
    qs, kr, dd, dsb, km, acc, grad, keep, home, pair, relay, mix,
    s_sem, l_sem, f_sem, c_send, c_recv, st_send, st_recv, d_send, y_send, y_recv,
    x_send, x_recv, h_send, h_recv, z_send, z_recv,
):
    f32, bf16 = jnp.float32, jnp.bfloat16
    g = lax.axis_index("grp")
    me = lax.axis_index("ulys")
    heads_all, rows = lse_hbm.shape
    heads = heads_all // CORES
    chunks = in_buf.shape[0]
    width = chunks * LANES
    per_chunk = LANES // head_dim
    half = head_dim // 2
    slots = CORES + 1
    span = slots * rows
    inputs = (q_ref, k_ref, v_ref, d_ref)

    c = lax.rem(me, CORES)
    yc = me // CORES
    far, near = yc, 1 - yc
    sib = me + 1 - 2 * c
    opp_base = CORES * (1 - yc)
    mate_base = CORES * yc
    is_near, is_far = c == near, c == far

    even = lax.rem(g, 2) == 0
    partner = jnp.where(even, g + 1, g - 1)
    up, down = g + 2, g - 2
    has_up, has_down = up < groups, down >= 0
    z_to = jnp.where(even, up, down)
    z_back = jnp.where(even, down, up)
    has_to = jnp.where(even, has_up, has_down)
    has_from = jnp.where(even, has_down, has_up)

    barrier = pltpu.get_barrier_semaphore()
    peers = [(g, sib)] + [(g, opp_base + o) for o in range(CORES)]
    peers += [(partner, mate_base + o) for o in range(CORES)]
    for peer in peers:
        pl.semaphore_signal(barrier, inc=1, device_id=peer, device_id_type=MESH)

    @pl.when(has_up)
    def _():
        pl.semaphore_signal(barrier, inc=1, device_id=(up, me), device_id_type=MESH)

    @pl.when(has_down)
    def _():
        pl.semaphore_signal(barrier, inc=1, device_id=(down, me), device_id_type=MESH)

    def load(p, t, other):
        w = 1 - c if other else c
        dst = stage.at[p, t] if other else in_buf.at[p, c, t]
        return pltpu.make_async_copy(
            inputs[t].at[:, pl.ds(pl.multiple_of(w * width + p * LANES, LANES), LANES)],
            dst, l_sem.at[p, t, int(other)],
        )

    def load_f(other):
        w = 1 - c if other else c
        return pltpu.make_async_copy(
            f_ref.at[:, pl.ds(pl.multiple_of(w * width, LANES), width)], f_vm.at[int(other)], f_sem.at[int(other)],
        )

    def remote(src, dst, send, recv, to):
        return pltpu.make_async_remote_copy(
            src_ref=src, dst_ref=dst, send_sem=send, recv_sem=recv, device_id=to, device_id_type=MESH,
        )

    def core_copy(p, slot):
        return remote(stage.at[p], in_buf.at[p, slot], c_send.at[p], c_recv.at[p], (g, sib))

    def first_copy(m, other):
        src = stage.at[m] if other else in_buf.at[m, c]
        to = 1 - c if other else c
        return remote(src, y_in.at[m], d_send.at[m, int(other)], y_recv.at[m], (g, opp_base + to))

    def y_copy(p):
        return remote(y_out.at[p], y_in.at[p + lag], y_send.at[p], y_recv.at[p + lag], (g, opp_base + c))

    def y_arrival(m):
        return remote(y_out.at[0], y_in.at[m], y_send.at[0], y_recv.at[m], (g, opp_base + c))

    def y_last_arrival(m):
        keep_to = pl.ds(0, GRADS)
        return remote(
            y_out.at[0, keep_to], y_in.at[m, keep_to], y_send.at[0], y_recv.at[m], (g, opp_base + c)
        )

    def y_last(p):
        return remote(
            y_out.at[p, pl.ds(0, GRADS)], y_in.at[p + lag, pl.ds(0, GRADS)],
            y_send.at[p], y_recv.at[p + lag], (g, opp_base + c),
        )

    def stat_core(slot):
        return remote(stat_oth, stat_in.at[slot], st_send.at[0], st_recv.at[slot], (g, sib))

    def stat_far(other):
        src = stat_oth if other else stat_in.at[c]
        to = 1 - c if other else c
        return remote(src, stat_in.at[CORES], st_send.at[1 + int(other)], st_recv.at[CORES], (g, opp_base + to))

    def x_copy(p, slot, kind, h):
        return remote(
            grad.at[p, slot], pair.at[h, p], x_send.at[kind, p], x_recv.at[h, p], (partner, mate_base + slot),
        )

    def home_copy(p, h):
        return remote(grad.at[p, 1 - c], home.at[h, p], h_send.at[p], h_recv.at[p], (g, sib))

    def x_late(h, p):
        return remote(mix.at[h, p - early], pair.at[h, p], x_send.at[h, p], x_recv.at[h, p], (partner, me))

    def z_late(h, p):
        return remote(home.at[h, p], relay.at[h, p], z_send.at[h, p], z_recv.at[h, p], (z_back, me))

    def z_copy(h, p):
        return remote(pair.at[h, p], relay.at[h, p], z_send.at[h, p], z_recv.at[h, p], (z_to, me))

    small = [
        pltpu.make_async_copy(src, dst, s_sem.at[i])
        for i, (src, dst) in enumerate(
            ((len_hbm, len_ref), (freq_hbm, freq_ref), (plan_hbm, plan_ref), (lse_hbm, lse_ref))
        )
    ]
    small[0].start()
    small[1].start()
    for t in range(INPUTS):
        for other in (False, True):
            load(0, t, other).start()
    load_f(False).start()
    load_f(True).start()
    for t in reversed(range(INPUTS)):
        for p in range(1, chunks):
            for other in (False, True):
                load(p, t, other).start()
        if t == INPUTS - 1:
            small[2].start()
            small[3].start()
    small[0].wait()
    small[1].wait()

    lengths = [len_ref[0, s] for s in range(len_ref.shape[1])]
    ends = []
    for s, length in enumerate(lengths):
        ends.append(length if s == 0 else ends[-1] + length)
    cut = sum(jnp.where(e <= CORES * rows, n, 0) for e, n in zip(ends, lengths))
    ship = jnp.where(cut >= rows, 1 - yc, yc)
    lane = lax.broadcasted_iota(jnp.int32, (rows, LANES), 1)
    low = lax.rem(lane, head_dim) < half
    shipping = jnp.full((rows, LANES), ship, jnp.int32) == 1

    def segments(index):
        return sum((index >= e).astype(jnp.int32) for e in ends)

    other_at = (2 - yc) * rows
    own_at = mate_base * rows
    group = lane // half
    row = lax.broadcasted_iota(jnp.int32, (rows, LANES), 0)
    row = jnp.where(group < CORES, own_at + group * rows, other_at) + row
    start = sum(jnp.where(row >= e, n, 0) for e, n in zip(ends, lengths))
    angle = (row - start).astype(f32) * freq_ref[...]
    for s, value in enumerate(spread(jnp.cos(angle), slots, half)):
        cos_t[s] = value
    for s, value in enumerate(spread(jnp.sin(angle), slots, half)):
        sin_t[s] = jnp.where(low, -value, value)

    col = lax.broadcasted_iota(jnp.int32, (1, span), 1)
    own_col = col < CORES * rows
    seg_i = segments(jnp.where(own_col, own_at + col, other_at - CORES * rows + col))
    sent = jnp.full((1, span), ship, jnp.int32) == 1
    for s in range(slots):
        at = own_at + s * rows if s < CORES else other_at
        seg_j = segments(lax.broadcasted_iota(jnp.int32, (rows, 1), 0) + at)
        if s < CORES:
            same = seg_j == jnp.where(own_col, seg_i, jnp.where(sent, -1, seg_i))
        else:
            same = seg_j == jnp.where(own_col, jnp.where(sent, -1, seg_i), -1)
        bias[s] = jnp.where(same, 0.0, -1e30)

    for t in range(INPUTS):
        for other in (False, True):
            load(0, t, other).wait()
    pl.semaphore_wait(barrier, len(peers) + has_up.astype(jnp.int32) + has_down.astype(jnp.int32))

    @pl.when(is_near)
    def _():
        first_copy(0, False).start()

    core_copy(0, c).start()
    small[2].wait()
    small[3].wait()

    for p in range(1, chunks):
        for other in (False, True):
            load(p, INPUTS - 1, other).wait()
    for other in (False, True):
        load_f(other).wait()
    owner = lax.broadcasted_iota(jnp.int32, (heads, width), 1) - head_dim * lax.broadcasted_iota(
        jnp.int32, (heads, width), 0
    )
    pick = jnp.where((owner >= 0) & (owner < head_dim), 1.0, 0.0).astype(bf16)
    for other in (True, False):
        if other:
            tiles = [stage[p, INPUTS - 1] for p in range(chunks)]
        else:
            tiles = [in_buf[p, c, INPUTS - 1] for p in range(chunks)]
        prod = jnp.concatenate(tiles, axis=1).astype(f32) * f_vm[int(other)].astype(f32)
        high = prod.astype(bf16)
        rest = (prod - high.astype(f32)).astype(bf16)
        delta = lax.dot_general(pick, high, NT, preferred_element_type=f32)
        delta += lax.dot_general(pick, rest, NT, preferred_element_type=f32)
        w = 1 - c if other else c
        lse = lse_ref[pl.ds(pl.multiple_of(w * heads, heads), heads), :]
        if other:
            stat_oth[0] = lse
            stat_oth[1] = delta
        else:
            stat_in[c, 0] = lse
            stat_in[c, 1] = delta
    stat_core(c).start()

    @pl.when(is_near)
    def _():
        stat_far(False).start()
        stat_far(True).start()
        first_copy(0, True).start()

    for p in range(1, chunks):
        for t in range(INPUTS - 1):
            for other in (False, True):
                load(p, t, other).wait()
        if p < lag:
            @pl.when(is_near)
            def _(p=p):
                first_copy(p, False).start()
                first_copy(p, True).start()

        core_copy(p, c).start()

    for idle, chosen in ((has_from, slice(0, early)), (has_to, slice(early, chunks))):
        @pl.when(jnp.logical_not(idle))
        def _(chosen=chosen):
            for h in range(CORES):
                relay[h, chosen] = jnp.zeros_like(relay[h, chosen])

    stat_core(1 - c).wait_recv()
    stat_far(False).wait_recv()
    for s in range(slots):
        stat[:, :, s * rows:(s + 1) * rows] = stat_in[s]
    for p in range(min(lag, chunks)):
        core_copy(p, 1 - c).wait_recv()

    head_of = lax.broadcasted_iota(jnp.int32, (1, LANES), 1) // head_dim

    def turn_back(x, s):
        return x * cos_t[s] - swap_halves(x, low, half) * sin_t[s]

    def compute(p):
        for s in range(slots):
            at = slice(s * rows, (s + 1) * rows)

            def take(t):
                return in_buf[p, s, t] if s < CORES else y_in[p, t]

            for t, out in ((0, qs), (1, kr)):
                x = take(t).astype(f32)
                y = (x * cos_t[s] + swap_halves(x, low, half) * sin_t[s]).astype(bf16)
                out[at, :] = y * 0.125 if t == 0 else y
            dd[at, :] = take(3)
        shares = []
        for s in range(slots):
            k_blk = kr[s * rows:(s + 1) * rows, :]
            v_blk = in_buf[p, s, 2] if s < CORES else y_in[p, 2]
            q_all, d_all = qs[...], dd[...]
            gv = jnp.zeros((rows, LANES), f32)
            gk = jnp.zeros((rows, LANES), f32)
            for a in range(per_chunk):
                mine = head_of == a
                q_a = jnp.where(mine, q_all, 0)
                d_a = jnp.where(mine, d_all, 0)
                at = slice((s * per_chunk + a) * rows, (s * per_chunk + a + 1) * rows)
                km[at, :] = jnp.where(mine, k_blk, 0)
                h = pl.ds(p * per_chunk + a, 1)
                score = lax.dot_general(k_blk, q_a, NT, preferred_element_type=f32)
                prob = jnp.exp(score + bias[s] - stat[0, h, :])
                dp = lax.dot_general(v_blk, d_a, NT, preferred_element_type=f32)
                ds = (prob * (dp - stat[1, h, :])).astype(bf16)
                gv += jnp.dot(prob.astype(bf16), d_a, preferred_element_type=f32)
                gk += jnp.dot(ds, q_a, preferred_element_type=f32)
                dsb[at, :] = ds
            gk = turn_back(gk, s)
            if s < CORES:
                acc[s, 1] = gk
                acc[s, 2] = gv
            else:
                shares = [gk, gv]
        dq = lax.dot_general(dsb[...], km[...], TN, preferred_element_type=f32) * 0.125
        for s in range(slots):
            part = turn_back(dq[s * rows:(s + 1) * rows, :], s)
            if s < CORES:
                acc[s, 0] = part
            else:
                shares = [part] + shares
        m = jnp.minimum(p + lag, chunks - 1)
        for t in range(GRADS):
            y_out[p, t] = jnp.where(shipping, in_buf[m, near, t], shares[t].astype(bf16))
        y_out[p, 3] = in_buf[m, near, 3]

        @pl.when(p + lag < chunks)
        def _():
            y_copy(p).start()

        @pl.when(p + lag >= chunks)
        def _():
            y_last(p).start()

        for t in range(GRADS):
            grad[p, far, t] = acc[far, t].astype(bf16)
            keep[p, t] = acc[near, t]

    def hand_on(p, slot, kind):
        @pl.when(p < early)
        def _():
            x_copy(p, slot, kind, c).start()

        @pl.when(c == slot)
        def _():
            home[c, p] = grad[p, slot]

        @pl.when(c != slot)
        def _():
            home_copy(p, c).start()

    offset = jnp.full((rows, LANES), plan_ref[0, me], jnp.int32)
    toward = jnp.where(even, 1, -1)
    stay, beside = offset == 0, offset == toward
    base = jnp.where(is_far, 0, lag)

    def deliver(q):
        @pl.when(q < early)
        def _():
            home_copy(q, 1 - c).wait_recv()

        for h in range(CORES):
            @pl.when((q < early) & has_from)
            def _(h=h):
                z_copy(h, q).wait_recv()

            @pl.when(q >= early)
            def _(h=h):
                x_late(h, q).wait_recv()

            near_by = beside | (jnp.full((rows, LANES), q, jnp.int32) >= early)
            at = pl.ds(pl.multiple_of((h * chunks + q) * LANES, LANES), LANES)
            for t, out in enumerate((oq_ref, ok_ref, ov_ref)):
                out[:, at] = jnp.where(stay, home[h, q, t], jnp.where(near_by, pair[h, q, t], relay[h, q, t]))

    def step(p, carry):
        @pl.when(p + lag < chunks)
        def _():
            core_copy(p + lag, 1 - c).wait_recv()

        @pl.when(p < chunks)
        def _():
            y_arrival(p).wait_recv()

        @pl.when((p >= chunks) & (p < chunks + lag))
        def _():
            y_last_arrival(p).wait_recv()

        @pl.when((p >= lag) & (p < chunks + lag))
        def _():
            q = p - lag
            for t in range(GRADS):
                got = jnp.where(shipping, y_in[p, t].astype(f32), 0.0)
                grad[q, near, t] = (keep[q, t] + got).astype(bf16)
            hand_on(q, near, 1)

        @pl.when(p < chunks)
        def _():
            compute(p)
            hand_on(p, far, 0)

        give = p - base - jnp.where(is_far, 1, 0)

        @pl.when((give >= early) & (give < chunks))
        def _():
            home_copy(give, 1 - c).wait_recv()

            @pl.when(has_from)
            def _():
                for h in range(CORES):
                    z_late(h, give).start()

        cross = give - 1

        @pl.when((cross >= early) & (cross < chunks))
        def _():
            for h in range(CORES):
                @pl.when(has_to)
                def _(h=h):
                    z_late(h, cross).wait_recv()

                for t in range(GRADS):
                    mix[h, cross - early, t] = jnp.where(beside, home[h, cross, t], relay[h, cross, t])
                x_late(h, cross).start()

        pass_on = p - base - RELAY

        @pl.when((pass_on >= 0) & (pass_on < early))
        def _():
            for h in range(CORES):
                x_copy(pass_on, c, 0, h).wait_recv()

                @pl.when(has_to)
                def _(h=h):
                    z_copy(h, pass_on).start()

        done = pass_on - 2

        @pl.when((done >= 0) & (done < chunks))
        def _():
            deliver(done)

        return carry

    lax.fori_loop(0, chunks + lag + RELAY + 2, step, 0)

    stat_core(c).wait_send()

    @pl.when(is_near)
    def _():
        for other in (False, True):
            stat_far(other).wait_send()
            for m in range(lag):
                first_copy(m, other).wait_send()

    def drain(p, carry):
        core_copy(p, c).wait_send()

        @pl.when(p + lag < chunks)
        def _():
            y_copy(p).wait_send()

        @pl.when(p + lag >= chunks)
        def _():
            y_last(p).wait_send()

        home_copy(p, c).wait_send()

        @pl.when(p < early)
        def _():
            x_copy(p, far, 0, c).wait_send()
            x_copy(p, near, 1, c).wait_send()

        @pl.when((p < early) & has_to)
        def _():
            for h in range(CORES):
                z_copy(h, p).wait_send()

        @pl.when(p >= early)
        def _():
            for h in range(CORES):
                x_late(h, p).wait_send()

        @pl.when((p >= early) & has_from)
        def _():
            for h in range(CORES):
                z_late(h, p).wait_send()

        return carry

    lax.fori_loop(0, chunks, drain, 0)


def per_device_halves(n, groups, query_in, key_in, value_in, grad_out, fwd_out, log_norm, sample_len, plan_offset):
    rows, cols = query_in.shape
    heads_all = log_norm.shape[1]
    head_dim = cols // heads_all
    half = head_dim // 2
    chunks = cols // CORES // LANES
    heads = heads_all // CORES
    slots = CORES + 1
    per_chunk = LANES // head_dim
    lag = min(LAG, chunks)
    early = max(chunks - LATE, 1)
    freq = np.power(10000.0, -np.arange(half) / half).astype(np.float32)
    freq = jnp.asarray(np.tile(freq, LANES // half)[None, :])
    bf16, f32 = jnp.bfloat16, jnp.float32
    vmem = pl.BlockSpec(memory_space=pltpu.VMEM)
    hbm = pl.BlockSpec(memory_space=pl.ANY)
    dma = pltpu.SemaphoreType.DMA
    return pl.pallas_call(
        functools.partial(halves_kernel, groups, head_dim, lag, early),
        out_shape=(pltpu.VMEM((rows, cols), bf16),) * 3,
        in_specs=[hbm] * 9,
        out_specs=(vmem, vmem, vmem),
        scratch_shapes=[
            pltpu.VMEM((1, LANES), f32),
            pltpu.SMEM(sample_len.shape, jnp.int32),
            pltpu.SMEM(plan_offset.shape, jnp.int32),
            pltpu.VMEM((heads_all, rows), f32),
            pltpu.VMEM((chunks, CORES, INPUTS, rows, LANES), bf16),
            pltpu.VMEM((chunks, INPUTS, rows, LANES), bf16),
            pltpu.VMEM((CORES, rows, cols // CORES), bf16),
            pltpu.VMEM((chunks + lag, INPUTS, rows, LANES), bf16),
            pltpu.VMEM((chunks, INPUTS, rows, LANES), bf16),
            pltpu.VMEM((2, heads, rows), f32),
            pltpu.VMEM((slots, 2, heads, rows), f32),
            pltpu.VMEM((2, heads, slots * rows), f32),
            pltpu.VMEM((slots, rows, LANES), f32),
            pltpu.VMEM((slots, rows, LANES), f32),
            pltpu.VMEM((slots, rows, slots * rows), f32),
            pltpu.VMEM((slots * rows, LANES), bf16),
            pltpu.VMEM((slots * rows, LANES), bf16),
            pltpu.VMEM((slots * rows, LANES), bf16),
            pltpu.VMEM((slots * per_chunk * rows, slots * rows), bf16),
            pltpu.VMEM((slots * per_chunk * rows, LANES), bf16),
            pltpu.VMEM((CORES, GRADS, rows, LANES), f32),
            pltpu.VMEM((chunks, CORES, GRADS, rows, LANES), bf16),
            pltpu.VMEM((chunks, GRADS, rows, LANES), f32),
            pltpu.VMEM((CORES, chunks, GRADS, rows, LANES), bf16),
            pltpu.VMEM((CORES, chunks, GRADS, rows, LANES), bf16),
            pltpu.VMEM((CORES, chunks, GRADS, rows, LANES), bf16),
            pltpu.VMEM((CORES, chunks - early, GRADS, rows, LANES), bf16),
            dma((4,)),
            dma((chunks, INPUTS, 2)),
            dma((2,)),
            dma((chunks,)),
            dma((chunks,)),
            dma((3,)),
            dma((slots,)),
            dma((lag, 2)),
            dma((chunks,)),
            dma((chunks + lag,)),
            dma((2, chunks)),
            dma((CORES, chunks)),
            dma((chunks,)),
            dma((chunks,)),
            dma((CORES, chunks)),
            dma((CORES, chunks)),
        ],
        compiler_params=pltpu.CompilerParams(collective_id=0, has_side_effects=True),
    )(freq, sample_len, plan_offset, log_norm.T, query_in, key_in, value_in, grad_out, fwd_out)


def solution(mesh):
    tokens = P(("grp", "ulys"), None)
    in_specs = (tokens,) * 6 + (P("grp", None), P("grp", None))
    n = mesh.shape["ulys"]
    two_chips = n == 2 * CORES
    body = functools.partial(per_device_halves if two_chips else per_device, n, mesh.shape["grp"])
    return jax.shard_map(
        body, mesh=mesh, in_specs=in_specs, out_specs=(tokens,) * 3, check_vma=False
    )
```
